256 devices in a mesh: doc: 4 (over x), ctx: 16 (over z, core), head: 4 (over y).
Axes of the slice: x: 4, y: 4, z: 8, core: 2. Of those that a mesh axis runs over, the one named last changes fastest.
Arguments:
- queries: bfloat16 [1024, 16384], P(('doc', 'ctx'), 'head'), as said below
- doc_of: int32 [1024, 1], P(('doc', 'ctx')), may hold values from 0 to 3; in each aligned block of 16 rows (0 to 15, 16 to 31, ...) at most 6 rows name the same one
- doc_lengths: int32 [4], replicated, may hold values from 4096 to 16384, as said below
- rotated_key_levels: bfloat16 [4, 16384, 1024], P('doc', 'ctx', 'head'), may hold values from -8 to 7
- rotated_value_levels: bfloat16 [4, 16384, 1024], P('doc', 'ctx', 'head'), may hold values from -8 to 7
- key_level_scale: bfloat16 [4, 8, 16384], P('doc', 'head', 'ctx'), may hold values from 0.19921875 to 0.796875
- value_level_scale: bfloat16 [4, 8, 16384], P('doc', 'head', 'ctx'), may hold values from 0.099609375 to 0.3984375
Outputs:
- attended: bfloat16 [1024, 16384], P(('doc', 'ctx'))
The draws below stay inside these ranges and needn't reach their ends.
Inputs may be any that keep to these rules, and one draw needn't show every extreme that they name: `queries`: query rows. `doc_of`: in the rows of one device no document is named by more than 6 requests, a bound that some block reaches. `doc_lengths`: some document is valid over all its positions.
All inputs are finite; a program needn't handle non-finite values.
Results may differ from the reference program's by a relative error of at most 0.02.
Values may be sent and summed in bfloat16 or wider, within the bound.
A program may use at most 128 MiB of HBM per device.

```python
import math
import jax
import jax.numpy as jnp
import numpy as np
from jax import lax

QUERY_HEADS = 128
KEY_VALUE_HEADS = 8
HEAD_WIDTH = 128
REQ_DEV = 16
CAP = 6
DOCUMENT_COUNT = 4
TOKEN_POSITIONS = 16384
REQ = 1024


def draw_queries(key, part):
    base = jnp.clip(jax.random.normal(key, (REQ, QUERY_HEADS * HEAD_WIDTH), jnp.float32), -6.0, 6.0)
    return base.astype(jnp.bfloat16)


def draw_doc_lengths(key, part):
    first = jax.random.fold_in(key, 11)
    second = jax.random.fold_in(key, 12)
    drawn = jax.random.randint(first, (DOCUMENT_COUNT,), TOKEN_POSITIONS // 4, TOKEN_POSITIONS + 1, jnp.int32)
    full_doc = jax.random.randint(second, (), 0, DOCUMENT_COUNT, jnp.int32)
    return jnp.where(jnp.arange(DOCUMENT_COUNT, dtype=jnp.int32) == full_doc, jnp.int32(TOKEN_POSITIONS), drawn).astype(jnp.int32)


def draw_rotated_key_levels(key, part):
    integer_levels = jax.random.randint(jax.random.fold_in(key, 21), (DOCUMENT_COUNT, TOKEN_POSITIONS, KEY_VALUE_HEADS * HEAD_WIDTH), -8, 8, jnp.int32)
    return integer_levels.astype(jnp.float32).astype(jnp.bfloat16)


def draw_rotated_value_levels(key, part):
    integer_levels = jax.random.randint(jax.random.fold_in(key, 22), (DOCUMENT_COUNT, TOKEN_POSITIONS, KEY_VALUE_HEADS * HEAD_WIDTH), -8, 8, jnp.int32)
    return integer_levels.astype(jnp.float32).astype(jnp.bfloat16)


def block_scale(key, dims, shards, smallest, largest):
    def one(axis_at, shards_of):
        draws = jax.random.uniform(jax.random.fold_in(jax.random.fold_in(key, 6), axis_at), (shards_of,), jnp.float32, smallest / len(shards), largest / len(shards))
        return jnp.repeat(jnp.exp(draws), dims[axis_at] // shards_of).reshape((-1,) + (1,) * (len(dims) - axis_at - 1))

    loudness = one(*shards[0])
    for cut in shards[1:]:
        loudness = loudness * one(*cut)
    return loudness


def shared_out(own_key, own, number, rows, amount, top, reach, skew):
    sequence = jax.random.permutation(own_key, amount)
    heavy_load, usual = load_shares(amount, rows * top, reach, skew, True), load_shares(amount, rows * top, reach, skew, False)
    places = jnp.arange(amount)

    def named(sizes, offset_by):
        used = int((sizes > 0).sum())
        fixed = max(1, used // 4)
        passed = fixed + (places - fixed + offset_by * (used - fixed)) % max(1, amount - fixed)
        return jnp.zeros((amount,), jnp.int32).at[sequence[jnp.where(places < fixed, places, passed)]].set(jnp.asarray(sizes, jnp.int32))

    sizes = jnp.where(number % 4 == 0, named(heavy_load, number // 4), named(usual, number - number // 4 - 1))
    mixed = jax.random.permutation(jax.random.fold_in(own, 3), amount)
    donor, taker = mixed[0:amount // 2 * 2:2], mixed[1:amount // 2 * 2:2]
    slack = jnp.minimum(sizes[donor] - 1, reach - sizes[taker]) // 2
    slack = jnp.where((donor == sequence[0]) | (taker == sequence[0]) | (sizes[taker] == 0), 0, jnp.maximum(slack, 0))
    passed = jax.random.randint(jax.random.fold_in(own, 4), (amount // 2,), 0, 1 << 20) % (slack + 1)
    sizes = sizes.at[donor].add(-passed).at[taker].add(passed)
    labels = jnp.searchsorted(jnp.cumsum(sizes), jnp.arange(rows * top), side="right").astype(jnp.int32)
    grid = labels.reshape(top, rows).T
    grid = grid[jax.random.permutation(jax.random.fold_in(own, 1), rows)]
    offset_by = jax.random.randint(jax.random.fold_in(own, 2), (rows, 1), 0, top)
    return jnp.take_along_axis(grid, (jnp.arange(top)[None, :] + offset_by) % top, axis=1)


def load_shares(count, total, reach, skew, full):
    weights = [(1 << 20) // math.isqrt(grade ** skew) + 1 for grade in range(1, count + 1)]
    largest = reach if full else min(reach, max(-(-total // count), total * weights[0] // sum(weights)))
    least = 1 if total - largest >= count - 1 else 0
    holding, surplus = [largest] + [least] * (count - 1), total - largest - least * (count - 1)
    while surplus > 0:
        candidates = [i for i in range(1, count) if holding[i] < largest] or [i for i in range(1, count) if holding[i] < reach]
        whole, left = sum([weights[i] for i in candidates]), surplus
        for i in candidates:
            extra = min(reach - holding[i], max(1, left * weights[i] // whole), surplus)
            holding[i] = holding[i] + extra
            surplus = surplus - extra
    return np.array(holding)


def setup_inputs(seed: int = 0) -> dict:
    key_list = jax.random.split(jax.random.key(seed), 8)
    queries = draw_queries(jax.random.fold_in(key_list[7], 71), 0)
    doc_of_keys = jax.random.split(jax.random.fold_in(key_list[1], 1), REQ // REQ_DEV)
    doc_of_turns = jax.random.permutation(jax.random.fold_in(key_list[1], 3), REQ // REQ_DEV)
    doc_of = jax.vmap(lambda own, number: shared_out(jax.random.fold_in(key_list[1], 2), own, number, REQ_DEV, DOCUMENT_COUNT, 1, CAP, 2))(doc_of_keys, doc_of_turns).reshape((REQ, 1))
    doc_lengths = draw_doc_lengths(jax.random.fold_in(key_list[7], 71), 0)
    rotated_key_levels = draw_rotated_key_levels(jax.random.fold_in(key_list[7], 71), 0)
    rotated_value_levels = draw_rotated_value_levels(jax.random.fold_in(key_list[7], 71), 0)
    key_level_scale = jnp.clip(jnp.exp(math.log(0.796875) - 1.3862944 * jax.random.uniform(key_list[5], (DOCUMENT_COUNT, KEY_VALUE_HEADS, TOKEN_POSITIONS), jnp.float32) ** block_scale(key_list[5], (DOCUMENT_COUNT, KEY_VALUE_HEADS, TOKEN_POSITIONS), ((0, 4), (1, 4), (2, 16)), -0.2, 0.2)), 0.19921875, 0.796875).astype(jnp.bfloat16)
    value_level_scale = jnp.clip(jnp.exp(math.log(0.3984375) - 1.3862944 * jax.random.uniform(key_list[6], (DOCUMENT_COUNT, KEY_VALUE_HEADS, TOKEN_POSITIONS), jnp.float32) ** block_scale(key_list[6], (DOCUMENT_COUNT, KEY_VALUE_HEADS, TOKEN_POSITIONS), ((0, 4), (1, 4), (2, 16)), -0.2, 0.2)), 0.099609375, 0.3984375).astype(jnp.bfloat16)
    return {"queries": queries, "doc_of": doc_of, "doc_lengths": doc_lengths, "rotated_key_levels": rotated_key_levels, "rotated_value_levels": rotated_value_levels, "key_level_scale": key_level_scale, "value_level_scale": value_level_scale}


def hadamard_signs():
    idx = jnp.arange(HEAD_WIDTH, dtype=jnp.int32)
    both = jnp.bitwise_and(idx[:, None], idx[None, :])
    parity = jnp.zeros_like(both)
    for bit in range(HEAD_WIDTH.bit_length()):
        parity = parity + jnp.bitwise_and(jnp.right_shift(both, bit), 1)
    return (1 - 2 * (parity % 2)).astype(jnp.float32)

def reference(queries, doc_of, doc_lengths, rotated_key_levels, rotated_value_levels, key_level_scale, value_level_scale):
    inverse_total = 1.0 / math.sqrt(HEAD_WIDTH)
    signs = hadamard_signs()
    head_group = QUERY_HEADS // KEY_VALUE_HEADS
    positions = jnp.arange(TOKEN_POSITIONS, dtype=jnp.int32)

    def single(item):
        query_row, document_index = item
        rotated_rows = (jnp.dot(query_row.reshape(QUERY_HEADS, HEAD_WIDTH), signs.astype(jnp.bfloat16), preferred_element_type=jnp.float32) * inverse_total).astype(jnp.bfloat16)
        rotated_rows = rotated_rows.astype(jnp.float32).reshape(KEY_VALUE_HEADS, head_group, HEAD_WIDTH)
        key_block = lax.dynamic_index_in_dim(rotated_key_levels, document_index, 0, keepdims=False).astype(jnp.float32).reshape(TOKEN_POSITIONS, KEY_VALUE_HEADS, HEAD_WIDTH)
        value_block = lax.dynamic_index_in_dim(rotated_value_levels, document_index, 0, keepdims=False).astype(jnp.float32).reshape(TOKEN_POSITIONS, KEY_VALUE_HEADS, HEAD_WIDTH)
        key_block_scale = lax.dynamic_index_in_dim(key_level_scale, document_index, 0, keepdims=False).astype(jnp.float32)
        value_block_scale = lax.dynamic_index_in_dim(value_level_scale, document_index, 0, keepdims=False).astype(jnp.float32)
        length = lax.dynamic_index_in_dim(doc_lengths, document_index, 0, keepdims=False)
        valid_mask = positions < length
        score_block = jnp.einsum('rpe,cre->rpc', rotated_rows, key_block, precision=lax.Precision.HIGHEST) * (key_block_scale * inverse_total)[:, None, :]
        score_block = jnp.where(valid_mask[None, None, :], score_block, jnp.float32(-1e+30))
        top = lax.optimization_barrier(jnp.max(score_block, axis=-1))
        probs = jnp.where(valid_mask[None, None, :], jnp.exp(score_block - top[..., None]), jnp.float32(0.0))
        total = lax.optimization_barrier(jnp.sum(probs, axis=-1))
        weights = (probs * value_block_scale[:, None, :]).astype(jnp.bfloat16).astype(jnp.float32)
        summed = jnp.einsum('kgs,skd->kgd', weights, value_block, precision=lax.Precision.HIGHEST)
        mixed = summed / total[..., None]
        result = jnp.einsum('kgd,de->kge', mixed, signs, precision=lax.Precision.HIGHEST) * inverse_total
        return result.astype(jnp.bfloat16).reshape(QUERY_HEADS * HEAD_WIDTH)
    return lax.map(single, (queries, doc_of[:, 0].astype(jnp.int32)))
```

```python
import functools
import math

import jax
import jax.numpy as jnp
import numpy as np
from jax import lax
from jax.experimental import pallas as pl
from jax.experimental.pallas import tpu as pltpu
from jax.sharding import PartitionSpec as P

HEAD_WIDTH = 128
GROUP = 16
SUBS = 2
MESH = pl.DeviceIdType.MESH
C = 1.0 / math.sqrt(HEAD_WIDTH)
LOG2E = math.log2(math.e)
F32 = jnp.float32
BF16 = jnp.bfloat16


def hadamard():
    i = np.arange(HEAD_WIDTH)
    both = i[:, None] & i[None, :]
    parity = np.zeros_like(both)
    for bit in range(7):
        parity ^= (both >> bit) & 1
    return (1 - 2 * parity).astype(np.float32)


def kernel(
    NX,
    NZ,
    NY,
    CAP,
    q_ref,
    doc_ref,
    len_ref,
    h_ref,
    ks_ref,
    vs_ref,
    k_ref,
    v_ref,
    out_ref,
    flat,
    rq,
    sendq,
    qbuf,
    kraw,
    vraw,
    ksb,
    vsb,
    kaug,
    vaug,
    sbuf,
    pacc,
    pmax,
    ptot,
    sacc,
    sml,
    racc,
    rml,
    fin,
    ret,
    obuf,
    loc_sem,
    kv_send,
    kv_recv,
    xq_send,
    xq_recv,
    ag_send,
    ag_recv,
    rs_send,
    rs_recv,
    rm_send,
    rm_recv,
    ret_send,
    ret_recv,
    y_send,
    y_recv,
):
    ix = lax.axis_index("doc")
    ic = lax.axis_index("ctx")
    iy = lax.axis_index("head")
    z, k = ic // 2, ic % 2
    L = NZ // 2
    rows = q_ref.shape[0]
    heads = q_ref.shape[1] // HEAD_WIDTH
    half_n = NX * CAP
    span = k_ref.shape[0]
    zp, zm = lax.rem(z + 1, NZ), lax.rem(z + NZ - 1, NZ)

    def dev(x, c, y):
        return (x, c, y)

    up, down = dev(ix, 2 * zp + k, iy), dev(ix, 2 * zm + k, iy)
    partner = dev(ix, 2 * z + (1 - k), iy)
    peers = [partner, up, down]
    for a in range(1, NX):
        for c in range(2):
            peers.append(dev(lax.rem(ix + a, NX), 2 * z + c, iy))
    for b in range(1, NY):
        peers.append(dev(ix, ic, lax.rem(iy + b, NY)))

    def remote(src, dst, ssem, rsem, device):
        return pltpu.make_async_remote_copy(
            src_ref=src,
            dst_ref=dst,
            send_sem=ssem,
            recv_sem=rsem,
            device_id=device,
            device_id_type=MESH,
        )

    own = pl.ds(pl.multiple_of(k * HEAD_WIDTH, HEAD_WIDTH), HEAD_WIDTH)
    other = pl.ds(pl.multiple_of((1 - k) * HEAD_WIDTH, HEAD_WIDTH), HEAD_WIDTH)
    local = [
        pltpu.make_async_copy(k_ref.at[:, own], kraw.at[k], loc_sem.at[0]),
        pltpu.make_async_copy(v_ref.at[:, own], vraw.at[k], loc_sem.at[1]),
        pltpu.make_async_copy(ks_ref, ksb.at[k], loc_sem.at[2]),
        pltpu.make_async_copy(vs_ref, vsb.at[k], loc_sem.at[3]),
    ]
    for copy in local:
        copy.start()

    barrier = pltpu.get_barrier_semaphore()
    for peer in peers:
        pl.semaphore_signal(barrier, inc=1, device_id=peer, device_id_type=MESH)

    for h in range(heads):
        flat[pl.ds(h, rows, stride=heads), :] = q_ref[
            :, h * HEAD_WIDTH : (h + 1) * HEAD_WIDTH
        ].astype(F32)
    signs = h_ref[...]
    rotated = jnp.dot(flat[...].astype(BF16), signs, preferred_element_type=F32) * F32(C)
    rq[...] = rotated.astype(BF16).reshape(rows, heads, HEAD_WIDTH)

    docs = [doc_ref[r, 0] for r in range(rows)]
    slots = []
    for r in range(rows):
        rank = jnp.int32(0)
        for e in range(r):
            rank = rank + jnp.where(docs[e] == docs[r], 1, 0)
        slots.append(docs[r] * CAP + rank)
    for d in range(NX):
        for s in range(CAP):
            at = jnp.int32(0)
            for r in range(1, rows):
                at = at + jnp.where(slots[r] == d * CAP + s, r, 0)
            request = rq[at]
            for g in range(2):
                sendq[d, g, s] = request[g * GROUP : (g + 1) * GROUP]

    pl.semaphore_wait(barrier, len(peers))

    mine = pl.ds(k * half_n + ix * CAP, CAP)
    xq = []
    for a in range(NX):
        for c in range(2):
            g = lax.rem(k + c, 2)
            xd = lax.rem(ix + a, NX)
            if a == 0 and c == 0:
                self_copy = pltpu.make_async_copy(
                    sendq.at[xd, g], qbuf.at[0, mine], loc_sem.at[4]
                )
                self_copy.start()
                continue
            copy = remote(
                sendq.at[xd, g],
                qbuf.at[0, mine],
                xq_send.at[a, c],
                xq_recv.at[a, c],
                dev(xd, 2 * z + g, iy),
            )
            copy.start()
            xq.append(copy)

    kv = [
        remote(k_ref.at[:, other], kraw.at[k], kv_send.at[0], kv_recv.at[0], partner),
        remote(v_ref.at[:, other], vraw.at[k], kv_send.at[1], kv_recv.at[1], partner),
        remote(ks_ref, ksb.at[k], kv_send.at[2], kv_recv.at[2], partner),
        remote(vs_ref, vsb.at[k], kv_send.at[3], kv_recv.at[3], partner),
    ]
    for copy in kv:
        copy.start()

    self_copy.wait()
    for copy in xq:
        copy.wait_recv()

    sub_n = half_n // SUBS

    def piece(h, u):
        return pl.ds(h * half_n + u * sub_n, sub_n)

    def forward(h, u, o_from, o_to, sem, device):
        return remote(
            qbuf.at[o_from, piece(h, u)],
            qbuf.at[o_to, piece(h, u)],
            ag_send.at[h, u, sem],
            ag_recv.at[h, u, o_to],
            device,
        )

    way = ((up, down), (down, up))
    for u in range(SUBS):
        for h in range(2):
            forward(h, u, 0, 1, 0, way[h][0]).start()
            if NZ - 1 > L:
                forward(h, u, 0, NZ - 1, NZ, way[h][1]).start()

    for copy in local:
        copy.wait()
    for copy in kv:
        copy.wait_recv()

    length = len_ref[ix]
    base = z * (2 * span)
    first = None
    for c in range(2):
        krow = jnp.where(k == 0, ksb[c].astype(F32)[0:1], ksb[c].astype(F32)[1:2])
        vrow = jnp.where(k == 0, vsb[c].astype(F32)[0:1], vsb[c].astype(F32)[1:2])
        krow = krow * F32(C * LOG2E)
        for j in range(span // 128):
            part = slice(j * 128, (j + 1) * 128)
            dest = slice(c * span + j * 128, c * span + (j + 1) * 128)
            start = base + c * span + j * 128
            scale = jnp.broadcast_to(krow[:, part], (128, 128)).T
            keys = kraw[c, part, :].astype(F32) * scale
            if first is None:
                first = keys[0:1]
            at = start + lax.broadcasted_iota(jnp.int32, (128, 128), 0)
            keys = jnp.where(at < length, keys, first)
            high = keys.astype(BF16)
            kaug[dest, 0:128] = high
            kaug[dest, 128:256] = (keys - high.astype(F32)).astype(BF16)
            at = start + lax.broadcasted_iota(jnp.int32, (128, 128), 1)
            values = vraw[c, part, :].astype(F32).T * vrow[:, part]
            vaug[0:128, dest] = jnp.where(at < length, values, 0.0).astype(BF16)
            vaug[128:144, dest] = jnp.where(at[0:16] < length, 1.0, 0.0).astype(BF16)

    tiles = 2 * half_n * GROUP // 256
    chunk = 256
    chunks = 2 * span // chunk

    def attend(o, tile):
        q = qbuf[o, pl.ds(tile * 16, 16)].reshape(256, HEAD_WIDTH)
        qq = jnp.concatenate([q, q], axis=1)
        top = None
        for i in range(chunks):
            part = slice(i * chunk, (i + 1) * chunk)
            s = lax.dot_general(
                kaug[part, :], qq, (((1,), (1,)), ((), ())), preferred_element_type=F32
            )
            sbuf[part, :] = s
            t = jnp.max(s.reshape(chunk // 8, 8, 256), axis=0)
            top = t if top is None else jnp.maximum(top, t)
        top = jnp.max(top, axis=0, keepdims=True)
        acc = None
        for i in range(chunks):
            part = slice(i * chunk, (i + 1) * chunk)
            p = jnp.exp2(sbuf[part, :] - top).astype(BF16)
            a = jnp.dot(vaug[:, part], p, preferred_element_type=F32)
            acc = a if acc is None else acc + a
        top = jnp.where(jnp.full((1, 256), base, jnp.int32) < length, top, F32(-1e30))
        for i in range(2):
            lanes = slice(i * 128, (i + 1) * 128)
            pacc[o, tile * 2 + i] = acc[0:128, lanes]
            ptot[o, tile * 2 + i] = acc[128:129, lanes]
            pmax[o, tile * 2 + i] = top[:, lanes]

    def attend_slot(o):
        @pl.loop(0, tiles)
        def _(tile):
            attend(o, tile)

    def gather_step(s, u):
        for h in range(2):
            forward(h, u, s, s, s, partner).wait_recv()

            @pl.when(s < L)
            def _():
                forward(h, u, s, s + 1, s, way[h][0]).start()

            @pl.when(s < NZ - L)
            def _():
                forward(h, u, NZ - s, NZ - s, 0, partner).wait_recv()

            @pl.when(s < NZ - L - 1)
            def _():
                forward(h, u, NZ - s, NZ - s - 1, NZ - s, way[h][1]).start()

    @pl.loop(1, L + 1)
    def _(s):
        count = jnp.where(s == 1, tiles, jnp.where(s == L, tiles, 2 * tiles))
        each = count // SUBS

        for u in range(SUBS):
            begin = u * each
            end = count if u == SUBS - 1 else (u + 1) * each

            def body(n, carry):
                o = jnp.where(n < tiles, jnp.where(s == 1, 0, NZ - s + 1), s - 1)
                attend(o, lax.rem(n, tiles))
                return carry

            lax.fori_loop(begin, end, body, 0)
            gather_step(s, u)

    groups = half_n * GROUP // 128

    def send_state(h, o_from, o_to, device):
        return (
            remote(
                sacc.at[h, o_from],
                racc.at[h, o_to],
                rs_send.at[h, o_from],
                rs_recv.at[h, o_to],
                device,
            ),
            remote(
                sml.at[h, o_from],
                rml.at[h, o_to],
                rm_send.at[h, o_from],
                rm_recv.at[h, o_to],
                device,
            ),
        )

    def wait_state(h, o):
        remote(sacc.at[h, 0], racc.at[h, o], rs_send.at[h, 0], rs_recv.at[h, o], partner).wait_recv()
        remote(sml.at[h, 0], rml.at[h, o], rm_send.at[h, 0], rm_recv.at[h, o], partner).wait_recv()

    def first_state(h, o, o_to, device):
        for g in range(groups):
            at = h * groups + g
            sacc[h, o, g] = pacc[o, at].astype(BF16)
            sml[h, o, g : g + 1] = pmax[o, at]
            sml[h, o, 4 + g : 5 + g] = ptot[o, at]
        for copy in send_state(h, o, o_to, device):
            copy.start()

    def merged(h, g, state, o_in):
        m1, l1, a1 = state
        m2 = rml[h, o_in, g : g + 1]
        l2 = rml[h, o_in, 4 + g : 5 + g]
        m = jnp.maximum(m1, m2)
        f1, f2 = jnp.exp2(m1 - m), jnp.exp2(m2 - m)
        return m, l1 * f1 + l2 * f2, a1 * f1 + racc[h, o_in, g].astype(F32) * f2

    def pass_on(h, o, o_to, device):
        wait_state(h, o)
        for g in range(groups):
            at = h * groups + g
            m, l, a = merged(h, g, (pmax[o, at], ptot[o, at], pacc[o, at]), o)
            sacc[h, o, g] = a.astype(BF16)
            sml[h, o, g : g + 1] = m
            sml[h, o, 4 + g : 5 + g] = l
        for copy in send_state(h, o, o_to, device):
            copy.start()

    if L + 1 < NZ:
        for h in range(2):
            first_state(h, L + 1, L + 2, way[h][0])
    attend_slot(L)
    for h in range(2):
        first_state(h, L, L - 1, way[h][1])
    if L > 1:
        attend_slot(L - 1)

    @pl.loop(0, L - 1)
    def _(n):
        s = L - 1 - n
        for h in range(2):
            pass_on(h, s, s - 1, way[h][1])

            @pl.when(s > 1)
            def _():
                o = NZ - s + 1
                pass_on(h, o, o + 1, way[h][0])

    for h in range(2):
        if NZ - 1 > L:
            wait_state(h, NZ)
        wait_state(h, 0)
        for g in range(groups):
            at = h * groups + g
            state = (pmax[0, at], ptot[0, at], pacc[0, at])
            if NZ - 1 > L:
                state = merged(h, g, state, NZ)
            _, l, a = merged(h, g, state, 0)
            x = a * (F32(C) / l)
            high = x.astype(BF16)
            low = (x - high.astype(F32)).astype(BF16)
            y = jnp.dot(signs, high, preferred_element_type=F32) + jnp.dot(
                signs, low, preferred_element_type=F32
            )
            fin[pl.ds(at * 8, 8)] = y.T.astype(BF16).reshape(8, GROUP, HEAD_WIDTH)

    returns = []
    for a in range(NX):
        for c in range(2):
            h = lax.rem(k + c, 2)
            xd = lax.rem(ix + a, NX)
            src = fin.at[pl.ds(h * half_n + xd * CAP, CAP)]
            dst = ret.at[pl.ds((ix * 2 + k) * CAP, CAP)]
            if a == 0 and c == 0:
                self_copy = pltpu.make_async_copy(src, dst, loc_sem.at[4])
                self_copy.start()
                continue
            copy = remote(
                src, dst, ret_send.at[a, c], ret_recv.at[a, c], dev(xd, 2 * z + h, iy)
            )
            copy.start()
            returns.append(copy)
    self_copy.wait()
    for copy in returns:
        copy.wait_recv()

    for r in range(rows):
        for g in range(2):
            at = (docs[r] * 2 + g) * CAP + (slots[r] - docs[r] * CAP)
            flat[r * heads + g * GROUP : r * heads + (g + 1) * GROUP, :] = ret[at].astype(F32)
    for h in range(heads):
        obuf[iy, :, h * HEAD_WIDTH : (h + 1) * HEAD_WIDTH] = flat[
            pl.ds(h, rows, stride=heads), :
        ].astype(BF16)

    width = q_ref.shape[1]

    def out_copy(y, sem):
        cols = pl.ds(pl.multiple_of(y * width, width), width)
        return pltpu.make_async_copy(obuf.at[y], out_ref.at[:, cols], loc_sem.at[5 + sem])

    outs = [out_copy(iy, 0)]
    outs[0].start()
    if NY > 1:
        yp, ym = lax.rem(iy + 1, NY), lax.rem(iy + NY - 1, NY)
        right, left = dev(ix, ic, yp), dev(ix, ic, ym)
        lanes = (slice(0, width // 2), slice(width // 2, width))

        def y_copy(y, part, sem, device):
            ref = obuf.at[y, :, lanes[part]]
            return remote(ref, ref, y_send.at[sem], y_recv.at[sem], device)

        sends = [
            y_copy(iy, 0, 0, right),
            y_copy(iy, 1, 1, left),
            y_copy(iy, 1, 2, right),
            y_copy(iy, 0, 3, left),
        ]
        for copy in sends:
            copy.start()
        y_copy(ym, 0, 0, right).wait_recv()
        relay = [y_copy(ym, 0, 4, right)]
        relay[0].start()
        y_copy(yp, 1, 1, left).wait_recv()
        relay.append(y_copy(yp, 1, 5, left))
        relay[1].start()
        y_copy(ym, 1, 2, right).wait_recv()
        outs.append(out_copy(ym, 1))
        outs[1].start()
        y_copy(yp, 0, 3, left).wait_recv()
        outs.append(out_copy(yp, 2))
        outs[2].start()
        far = lax.rem(iy + 2, NY)
        y_copy(far, 0, 4, right).wait_recv()
        y_copy(far, 1, 5, left).wait_recv()
        outs.append(out_copy(far, 3))
        outs[3].start()
        for copy in sends + relay:
            copy.wait_send()

    for copy in xq + kv + returns:
        copy.wait_send()
    for h in range(2):
        for u in range(SUBS):
            for o in range(0, L):
                forward(h, u, o, o + 1, o, way[h][0]).wait_send()
            for o in range(NZ, L + 1, -1):
                forward(h, u, o % NZ, o - 1, o, way[h][1]).wait_send()
        for o in range(1, L + 1):
            for copy in send_state(h, o, o - 1, way[h][1]):
                copy.wait_send()
        for o in range(L + 1, NZ):
            for copy in send_state(h, o, o + 1, way[h][0]):
                copy.wait_send()
    for copy in outs:
        copy.wait()


def shards(NX, NZ, NY, queries, doc_of, doc_lengths, keys, values, key_scale, value_scale):
    rows, width = queries.shape
    cap = max(2, 3 * rows // (2 * NX))
    heads = width // HEAD_WIDTH
    _, span, cols = keys.shape
    half_n = NX * cap
    groups = 2 * half_n * GROUP // 128
    vmem, smem = pltpu.VMEM, pltpu.SMEM
    dma = pltpu.SemaphoreType.DMA
    signs = jnp.asarray(hadamard(), BF16)
    any_spec = pl.BlockSpec(memory_space=pl.ANY)
    return pl.pallas_call(
        functools.partial(kernel, NX, NZ, NY, cap),
        out_shape=jax.ShapeDtypeStruct((rows, width * NY), BF16),
        in_specs=[
            pl.BlockSpec(memory_space=vmem),
            pl.BlockSpec(memory_space=smem),
            pl.BlockSpec(memory_space=smem),
            pl.BlockSpec(memory_space=vmem),
            pl.BlockSpec(memory_space=vmem),
            pl.BlockSpec(memory_space=vmem),
            any_spec,
            any_spec,
        ],
        out_specs=any_spec,
        scratch_shapes=[
            vmem((rows * heads, HEAD_WIDTH), F32),
            vmem((rows, heads, HEAD_WIDTH), BF16),
            vmem((NX, 2, cap, GROUP, HEAD_WIDTH), BF16),
            vmem((NZ, 2 * half_n, GROUP, HEAD_WIDTH), BF16),
            vmem((2, span, HEAD_WIDTH), BF16),
            vmem((2, span, HEAD_WIDTH), BF16),
            vmem((2, 2, span), BF16),
            vmem((2, 2, span), BF16),
            vmem((2 * span, 2 * HEAD_WIDTH), BF16),
            vmem((HEAD_WIDTH + 16, 2 * span), BF16),
            vmem((2 * span, 256), F32),
            vmem((NZ, groups, 128, 128), F32),
            vmem((NZ, groups, 1, 128), F32),
            vmem((NZ, groups, 1, 128), F32),
            vmem((2, NZ, groups // 2, 128, 128), BF16),
            vmem((2, NZ, 8, 128), F32),
            vmem((2, NZ + 1, groups // 2, 128, 128), BF16),
            vmem((2, NZ + 1, 8, 128), F32),
            vmem((2 * half_n, GROUP, HEAD_WIDTH), BF16),
            vmem((NX * 2 * cap, GROUP, HEAD_WIDTH), BF16),
            vmem((NY, rows, width), BF16),
            dma((9,)),
            dma((4,)),
            dma((4,)),
            dma((NX, 2)),
            dma((NX, 2)),
            dma((2, SUBS, NZ + 1)),
            dma((2, SUBS, NZ + 1)),
            dma((2, NZ + 1)),
            dma((2, NZ + 1)),
            dma((2, NZ + 1)),
            dma((2, NZ + 1)),
            dma((NX, 2)),
            dma((NX, 2)),
            dma((6,)),
            dma((6,)),
        ],
        compiler_params=pltpu.CompilerParams(
            collective_id=0, has_side_effects=True, vmem_limit_bytes=60 * 1024 * 1024
        ),
    )(
        queries,
        doc_of,
        doc_lengths,
        signs,
        key_scale[0],
        value_scale[0],
        keys[0],
        values[0],
    )


def solution(mesh):
    in_specs = (
        P(("doc", "ctx"), "head"),
        P(("doc", "ctx"), None),
        P(),
        P("doc", "ctx", "head"),
        P("doc", "ctx", "head"),
        P("doc", "head", "ctx"),
        P("doc", "head", "ctx"),
    )
    out_specs = P(("doc", "ctx"), None)
    sizes = (mesh.shape["doc"], mesh.shape["ctx"] // 2, mesh.shape["head"])
    return jax.shard_map(
        functools.partial(shards, *sizes),
        mesh=mesh,
        in_specs=in_specs,
        out_specs=out_specs,
        check_vma=False,
    )
```
